512 devices in a mesh: tm: 16 (over z, core), space: 32 (over y, x).
Axes of the slice: x: 4, y: 8, z: 8, core: 2. Of those that a mesh axis runs over, the one named last changes fastest.
Arguments:
- queries: bfloat16 [65536, 2560], P(('tm', 'space')), may hold values from -6 to 6
- keys: bfloat16 [65536, 2560], P(('tm', 'space')), may hold values from -6 to 6
- values: bfloat16 [65536, 2560], P(('tm', 'space')), may hold values from -6 to 6
- grad_out: bfloat16 [65536, 2560], P(('tm', 'space')), may hold values from -6 to 6
- saved_state: bfloat16 [16, 20, 128, 128], P('tm', None, 'space'), may hold values from -0.3984375 to 0.3984375
Outputs:
- grad_q: bfloat16 [65536, 2560], P(('tm', 'space'))
- grad_k: bfloat16 [65536, 2560], P(('tm', 'space'))
- grad_v: bfloat16 [65536, 2560], P(('tm', 'space'))
The draws below stay inside these ranges and needn't reach their ends.
All inputs are finite; a program needn't handle non-finite values.
Results may differ from the reference program's by a relative error of at most 0.0049.
Values may be sent and summed in bfloat16 or wider, within the bound.
A program may use at most 64 MiB of HBM per device.

```python
import math
import jax
import jax.numpy as jnp
from jax import lax

HEADS = 20
HD = 128
WIDTH = 2560
BLOCKS = 16
BLOCK_TOK = 4096
TOKENS = 65536


def block_scale(own_key, extent, cuts, smallest, top_value):
    def one(position, shards_of):
        steps = jax.random.uniform(jax.random.fold_in(jax.random.fold_in(own_key, 6), position), (shards_of,), jnp.float32, smallest / len(cuts), top_value / len(cuts))
        return jnp.repeat(jnp.exp(steps), extent[position] // shards_of).reshape((-1,) + (1,) * (len(extent) - position - 1))

    level = one(*cuts[0])
    for cut in cuts[1:]:
        level = level * one(*cut)
    return level


def noise(rng, dims, scale, bound, cuts=(), held_as=jnp.bfloat16):
    drawn = scale * jax.random.normal(rng, dims, jnp.float32)
    if cuts:
        drawn = drawn * block_scale(rng, dims, cuts, -0.22, 0.18)
    return jnp.clip(drawn, -bound, bound).astype(held_as)


def setup_inputs(seed: int = 0) -> dict:
    arg_keys = jax.random.split(jax.random.key(seed), 6)
    return {
        "queries": noise(arg_keys[0], (TOKENS, WIDTH), 1.0, 6.0, ((0, 512),)),
        "keys": noise(arg_keys[1], (TOKENS, WIDTH), 1.0, 6.0, ((0, 512),)),
        "values": noise(arg_keys[2], (TOKENS, WIDTH), 1.0, 6.0, ((0, 512),)),
        "grad_out": noise(arg_keys[3], (TOKENS, WIDTH), 1.0, 6.0, ((0, 512),)),
        "saved_state": noise(arg_keys[4], (BLOCKS, HEADS, HD, HD), 0.05, 0.3984375, ((0, 16), (2, 32))),
    }


def block_partial(pair):
    q_block, out_block = pair
    scale = 1.0 / math.sqrt(TOKENS * HD)
    q_feat = jnp.maximum(q_block, 0).astype(jnp.float32)
    return scale * jnp.einsum('thd,the->hde', q_feat, out_block.astype(jnp.float32))

def block_grads(items):
    q_block, k_block, v_block, out_block, state_block, grad_block = items
    state_f = state_block.astype(jnp.float32)
    grad_f = grad_block.astype(jnp.float32)
    dq_full = jnp.einsum('the,hde->thd', out_block.astype(jnp.float32), state_f)
    dq_out = jnp.where(q_block > 0, dq_full, 0.0).astype(jnp.bfloat16)
    dk_full = jnp.einsum('the,hde->thd', v_block.astype(jnp.float32), grad_f)
    dk_out = jnp.where(k_block > 0, dk_full, 0.0).astype(jnp.bfloat16)
    k_feat = jnp.maximum(k_block, 0).astype(jnp.float32)
    dv_out = jnp.einsum('thd,hde->the', k_feat, grad_f).astype(jnp.bfloat16)
    return (dq_out, dk_out, dv_out)

def reference(queries, keys, values, grad_out, saved_state):
    shape4 = (BLOCKS, BLOCK_TOK, HEADS, HD)
    q_all = queries.reshape(shape4)
    k_all = keys.reshape(shape4)
    v_all = values.reshape(shape4)
    o_all = grad_out.reshape(shape4)
    parts = lax.map(block_partial, (q_all, o_all))
    gsum = jnp.flip(jnp.cumsum(jnp.flip(parts, 0), axis=0), 0)
    gstate = gsum.astype(jnp.bfloat16)
    dq_all, dk_all, dv_all = lax.map(block_grads, (q_all, k_all, v_all, o_all, saved_state, gstate))
    return (dq_all.reshape(TOKENS, WIDTH), dk_all.reshape(TOKENS, WIDTH), dv_all.reshape(TOKENS, WIDTH))
```

```python
import functools
import math

import jax
import jax.numpy as jnp
from jax import lax
from jax.experimental import pallas as pl
from jax.experimental.pallas import tpu as pltpu
from jax.sharding import PartitionSpec as P

MESH = pl.DeviceIdType.MESH
F32 = jnp.float32
BF16 = jnp.bfloat16
NX, NY, NZ = 4, 8, 8
ROWS = 16
GROUPS = ((0, 1), (1, 1), (2, 1), (3, 1), (4, 1))
XS = (2, 1, 3)
RING = (4, 3, 5, 2, 6, 1, 7)


def nt(a, b):
    return lax.dot_general(a, b, (((1,), (1,)), ((), ())), preferred_element_type=F32)


def tn(a, b):
    return lax.dot_general(a, b, (((0,), (0,)), ((), ())), preferred_element_type=F32)


def nn(a, b):
    return lax.dot_general(a, b, (((1,), (0,)), ((), ())), preferred_element_type=F32)


def kernel(
    scale,
    q_hbm,
    k_hbm,
    v_hbm,
    o_hbm,
    s_hbm,
    dq,
    dk,
    dv,
    q,
    k,
    v,
    o,
    s_rows,
    part,
    own,
    from_x,
    summed,
    from_y,
    share,
    share_sum,
    from_core,
    pair,
    from_z,
    state,
    saved,
    select,
    load_sem,
    x_send,
    x_recv,
    y_send,
    y_recv,
    c_send,
    c_recv,
    z_send,
    z_recv,
    gy_send,
    gy_recv,
    gx_send,
    gx_recv,
    s_send,
    s_recv,
):
    heads, hd = state.shape[0], state.shape[2]
    steps = heads // NX
    tm, sp = lax.axis_index("tm"), lax.axis_index("space")
    z, c = lax.div(tm, 2), lax.rem(tm, 2)
    y, x = lax.div(sp, NX), lax.rem(sp, NX)

    x_at = {d: lax.rem(x + d, NX) for d in range(NX)}
    y_at = {d: lax.rem(y + d, NY) for d in range(1, NY)}
    to_x = {d: (tm, y * NX + x_at[d]) for d in XS}
    to_y = {d: (tm, y_at[d] * NX + x) for d in RING}
    rows_of = {d: pl.ds(pl.multiple_of(y_at[d] * ROWS, ROWS), ROWS) for d in RING}
    mine = pl.ds(pl.multiple_of(y * ROWS, ROWS), ROWS)
    other_core = (tm + 1 - 2 * c, sp)

    def remote(src, dst, send, recv, device):
        return pltpu.make_async_remote_copy(
            src_ref=src, dst_ref=dst, send_sem=send, recv_sem=recv, device_id=device, device_id_type=MESH
        )

    barrier = pltpu.get_barrier_semaphore()

    def greet(device):
        pl.semaphore_signal(barrier, inc=1, device_id=device, device_id_type=MESH)

    loads = [
        pltpu.make_async_copy(src, dst, load_sem.at[n])
        for n, (src, dst) in enumerate(((q_hbm, q), (o_hbm, o), (s_hbm, s_rows), (k_hbm, k), (v_hbm, v)))
    ]
    loads[0].start()
    loads[1].start()
    for d in RING:
        greet(to_y[d])

        @pl.when(d < NZ - z)
        def _(d=d):
            greet((tm + 2 * d, sp))

    for d in XS:
        greet(to_x[d])
    greet(other_core)
    for n in range(2, 5):
        loads[n].start()

    def column(h):
        return pl.ds(pl.multiple_of(h * hd, hd), hd)

    def span(g):
        first, count = GROUPS[g]
        return pl.ds(first, count)

    def own_heads(g):
        first, count = GROUPS[g]
        return pl.ds(x * steps + first, count)

    def send_x(g, d):
        return remote(part.at[d - 1, span(g)], from_x.at[d - 1, span(g)], x_send.at[g], x_recv.at[g], to_x[d])

    def all_x(g, send, recv):
        return remote(from_x.at[:, span(g)], from_x.at[:, span(g)], send.at[g], recv.at[g], to_x[1])

    def send_y(g, d):
        return remote(summed.at[span(g), rows_of[d]], from_y.at[d - 1, span(g)], y_send.at[g], y_recv.at[g], to_y[d])

    def all_y(g, send, recv):
        return remote(from_y.at[:, span(g)], from_y.at[:, span(g)], send.at[g], recv.at[g], to_y[1])

    def send_core(g):
        return remote(share.at[span(g)], from_core.at[span(g)], c_send.at[g], c_recv.at[g], other_core)

    def send_z(g, d):
        return remote(
            pair.at[span(g)], from_z.at[d - 1, span(g)], z_send.at[g, d - 1], z_recv.at[g, d - 1], (tm - 2 * d, sp)
        )

    def send_gy(g, d):
        piece = state.at[own_heads(g), mine]
        return remote(piece, piece, gy_send.at[g], gy_recv.at[g], to_y[d])

    def send_gx(g, d):
        piece = state.at[own_heads(g)]
        return remote(piece, piece, gx_send.at[g], gx_recv.at[g], to_x[d])

    def send_sy(d):
        piece = saved.at[y, x]
        return remote(piece, piece, s_send.at[0], s_recv.at[0], to_y[d])

    def send_sx(d):
        piece = saved.at[:, x]
        return remote(piece, piece, s_send.at[1], s_recv.at[1], to_x[d])

    def all_sy():
        piece = saved.at[pl.ds(0, NY - 1), 0]
        return remote(piece, piece, s_send.at[0], s_recv.at[0], to_y[1])

    def all_sx():
        piece = saved.at[:, pl.ds(0, NX - 1)]
        return remote(piece, piece, s_send.at[1], s_recv.at[1], to_x[1])

    def partial_states(g):
        first, count = GROUPS[g]
        for d in XS + (0,):
            for n in range(first, first + count):
                cols = column(x_at[d] * steps + n)
                product = tn(jnp.maximum(q[:, cols], 0), o[:, cols])
                if d:
                    part[d - 1, n] = product.astype(BF16)
                else:
                    own[n] = product

    loads[0].wait()
    loads[1].wait()
    for g in range(len(GROUPS)):
        partial_states(g)
    pl.semaphore_wait(barrier, NX - 1 + NY - 1 + 1 + z)
    for g in range(len(GROUPS)):
        for d in XS:
            send_x(g, d).start()

    loads[2].wait()
    for j in range(heads // 4):
        saved_rows = jnp.concatenate([s_rows[0, 4 * j + i].astype(F32) for i in range(4)], axis=0)
        saved[y, x, pl.ds(j * 16, 16), :] = saved_rows.astype(BF16)
    for d in RING:
        send_sy(d).start()

    row = lax.broadcasted_iota(jnp.int32, (hd, 4 * hd), 0)
    col = lax.broadcasted_iota(jnp.int32, (hd, 4 * hd), 1)
    target = (col // 16) * 4 + col % 4
    for i in range(4):
        hit = (row == target) & ((col // 4) % 4 == i)
        select[i] = jnp.where(hit, 1.0, 0.0).astype(BF16)

    for g, (first, count) in enumerate(GROUPS):
        all_x(g, x_send, x_recv).wait_recv()
        for n in range(first, first + count):
            total = own[n] + from_x[0, n].astype(F32) + from_x[1, n].astype(F32) + from_x[2, n].astype(F32)
            own[n] = total
            summed[n] = total.astype(BF16)
        for d in RING:
            send_y(g, d).start()

    all_sy().wait_recv()
    for d in XS:
        send_sx(d).start()

    def pass_down(g):
        send_core(g).wait_recv()
        ours, theirs = share[span(g)], from_core[span(g)]
        pair[span(g)] = (ours + theirs).astype(BF16)
        for d in RING:

            @pl.when(d <= z)
            def _(d=d):
                send_z(g, d).start()

        share_sum[span(g)] = ours + jnp.where(c == 0, theirs, 0.0)

    for g, (first, count) in enumerate(GROUPS):
        all_y(g, y_send, y_recv).wait_recv()
        for n in range(first, first + count):
            total = own[n, mine, :]
            for d in range(1, NY):
                total = total + from_y[d - 1, n].astype(F32)
            share[n] = total
        send_core(g).start()
        if g:
            pass_down(g - 1)
    pass_down(len(GROUPS) - 1)

    for g, (first, count) in enumerate(GROUPS):
        for d in range(1, NZ):

            @pl.when(d < NZ - z)
            def _(d=d, g=g):
                send_z(g, d).wait_recv()
                share_sum[span(g)] = share_sum[span(g)] + from_z[d - 1, span(g)].astype(F32)

        for n in range(first, first + count):
            state[x * steps + n, mine, :] = (scale * share_sum[n]).astype(BF16)
        for d in RING:
            send_gy(g, d).start()

    all_sx().wait_recv()

    def query_grads(j):
        rows = saved[:, :, pl.ds(j * 16, 16), :].reshape(4 * hd, hd)
        for i in range(4):
            h = 4 * j + i
            cols = slice(h * hd, (h + 1) * hd)
            matrix = nn(select[i], rows).astype(BF16)
            product = nt(o[:, cols], matrix)
            dq[:, cols] = jnp.where(q[:, cols].astype(F32) > 0, product, 0.0).astype(BF16)

    pieces = heads // 4
    for g in range(len(GROUPS)):
        for j in range(g * pieces // len(GROUPS), (g + 1) * pieces // len(GROUPS)):
            query_grads(j)
        all_y(g, gy_send, gy_recv).wait_recv()
        for d in XS:
            send_gx(g, d).start()

    loads[3].wait()
    loads[4].wait()
    for g, (first, count) in enumerate(GROUPS):
        all_x(g, gx_send, gx_recv).wait_recv()
        for n in range(first, first + count):
            for m in range(NX):
                h = m * steps + n
                cols = slice(h * hd, (h + 1) * hd)
                matrix = state[h]
                keys = k[:, cols]
                product = nt(v[:, cols], matrix)
                dk[:, cols] = jnp.where(keys.astype(F32) > 0, product, 0.0).astype(BF16)
                dv[:, cols] = nn(jnp.maximum(keys, 0), matrix).astype(BF16)

    for g in range(len(GROUPS)):
        all_x(g, x_send, x_recv).wait_send()
        all_y(g, y_send, y_recv).wait_send()
        send_core(g).wait_send()
        for d in RING:

            @pl.when(d <= z)
            def _(d=d, g=g):
                send_z(g, d).wait_send()

        all_y(g, gy_send, gy_recv).wait_send()
        all_x(g, gx_send, gx_recv).wait_send()
    all_sy().wait_send()
    all_sx().wait_send()


def store(a, b, c, a_hbm, b_hbm, c_hbm, sem):
    copies = [
        pltpu.make_async_copy(src, dst, sem.at[n]) for n, (src, dst) in enumerate(((a, a_hbm), (b, b_hbm), (c, c_hbm)))
    ]
    for copy in copies:
        copy.start()
    for copy in copies:
        copy.wait()


def per_device(queries, keys, values, grad_out, saved_state):
    tok, width = queries.shape
    heads, hd = saved_state.shape[1], saved_state.shape[3]
    steps = heads // NX
    total_tok = tok * lax.axis_size("tm") * lax.axis_size("space")
    scale = 1.0 / math.sqrt(total_tok * hd)
    dma = pltpu.SemaphoreType.DMA
    vmem = pltpu.VMEM
    anywhere = pl.BlockSpec(memory_space=pl.ANY)
    local = pl.BlockSpec(memory_space=vmem)
    out = jax.ShapeDtypeStruct((tok, width), BF16)
    groups = len(GROUPS)
    grads = pl.pallas_call(
        functools.partial(kernel, scale),
        out_shape=(out, out, out),
        in_specs=[anywhere] * 5,
        out_specs=(local, local, local),
        scratch_shapes=[vmem((tok, width), BF16)] * 4
        + [
            vmem(saved_state.shape, BF16),
            vmem((NX - 1, steps, hd, hd), BF16),
            vmem((steps, hd, hd), F32),
            vmem((NX - 1, steps, hd, hd), BF16),
            vmem((steps, hd, hd), BF16),
            vmem((NY - 1, steps, ROWS, hd), BF16),
            vmem((steps, ROWS, hd), F32),
            vmem((steps, ROWS, hd), F32),
            vmem((steps, ROWS, hd), F32),
            vmem((steps, ROWS, hd), BF16),
            vmem((NZ - 1, steps, ROWS, hd), BF16),
            vmem((heads, hd, hd), BF16),
            vmem((NY, NX, heads * 4, hd), BF16),
            vmem((4, hd, 4 * hd), BF16),
            dma((5,)),
            dma((groups,)),
            dma((groups,)),
            dma((groups,)),
            dma((groups,)),
            dma((groups,)),
            dma((groups,)),
            dma((groups, NZ - 1)),
            dma((groups, NZ - 1)),
            dma((groups,)),
            dma((groups,)),
            dma((groups,)),
            dma((groups,)),
            dma((2,)),
            dma((2,)),
        ],
        compiler_params=pltpu.CompilerParams(
            collective_id=0, has_side_effects=True, vmem_limit_bytes=24000 * 1024
        ),
        name="state_grads",
    )(*(pltpu.with_memory_space_constraint(a, pltpu.HBM) for a in (queries, keys, values, grad_out, saved_state)))
    return pl.pallas_call(
        store,
        out_shape=(out, out, out),
        in_specs=[anywhere] * 3,
        out_specs=(anywhere, anywhere, anywhere),
        scratch_shapes=[dma((3,))],
        compiler_params=pltpu.CompilerParams(vmem_limit_bytes=1024 * 1024),
        name="store_grads",
    )(*grads)


def solution(mesh):
    rows = P(("tm", "space"), None)
    return jax.shard_map(
        per_device,
        mesh=mesh,
        in_specs=(rows, rows, rows, rows, P("tm", None, "space", None)),
        out_specs=(rows, rows, rows),
        check_vma=False,
    )
```

```python
import functools
import math

import jax
import jax.numpy as jnp
from jax import lax
from jax.experimental import pallas as pl
from jax.experimental.pallas import tpu as pltpu
from jax.sharding import PartitionSpec as P

MESH = pl.DeviceIdType.MESH
F32 = jnp.float32
BF16 = jnp.bfloat16
NX, NY, NZ = 4, 8, 8
ROWS = 16
X_FIRST = (1,)
GROUPS = ((0, 1), (1, 1), (2, 1), (3, 1), (4, 1))
XS = (2, 1, 3)
RING = (4, 3, 5, 2, 6, 1, 7)


def nt(a, b):
    return lax.dot_general(a, b, (((1,), (1,)), ((), ())), preferred_element_type=F32)


def tn(a, b):
    return lax.dot_general(a, b, (((0,), (0,)), ((), ())), preferred_element_type=F32)


def nn(a, b):
    return lax.dot_general(a, b, (((1,), (0,)), ((), ())), preferred_element_type=F32)


def kernel(
    scale,
    q_hbm,
    k_hbm,
    v_hbm,
    o_hbm,
    s_hbm,
    dq,
    dk,
    dv,
    q,
    k,
    v,
    o,
    s_rows,
    part,
    own,
    from_x,
    summed,
    from_y,
    share,
    share_sum,
    from_core,
    pair,
    from_z,
    state,
    saved,
    select,
    load_sem,
    x_send,
    x_recv,
    y_send,
    y_recv,
    c_send,
    c_recv,
    z_send,
    z_recv,
    gy_send,
    gy_recv,
    gx_send,
    gx_recv,
    s_send,
    s_recv,
    ready,
):
    steps, hd = state.shape[1], state.shape[3]
    heads = NX * steps
    tm, sp = lax.axis_index("tm"), lax.axis_index("space")
    z, c = lax.div(tm, 2), lax.rem(tm, 2)
    y, x = lax.div(sp, NX), lax.rem(sp, NX)

    x_at = {d: lax.rem(x + d, NX) for d in range(NX)}
    y_at = {d: lax.rem(y + d, NY) for d in range(1, NY)}
    to_x = {d: (tm, y * NX + x_at[d]) for d in XS}
    to_y = {d: (tm, y_at[d] * NX + x) for d in RING}
    rows_of = {d: pl.ds(pl.multiple_of(y_at[d] * ROWS, ROWS), ROWS) for d in RING}
    mine = pl.ds(pl.multiple_of(y * ROWS, ROWS), ROWS)
    other_core = (tm + 1 - 2 * c, sp)

    def remote(src, dst, send, recv, device):
        return pltpu.make_async_remote_copy(
            src_ref=src, dst_ref=dst, send_sem=send, recv_sem=recv, device_id=device, device_id_type=MESH
        )

    barrier = pltpu.get_barrier_semaphore()

    def greet(device):
        pl.semaphore_signal(barrier, inc=1, device_id=device, device_id_type=MESH)

    loads = [
        pltpu.make_async_copy(src, dst, load_sem.at[n])
        for n, (src, dst) in enumerate(((q_hbm, q), (o_hbm, o), (s_hbm, s_rows), (k_hbm, k), (v_hbm, v)))
    ]
    loads[0].start()
    loads[1].start()
    for d in RING:
        if d in (1, 7):
            greet(to_y[d])

        @pl.when(d < NZ - z)
        def _(d=d):
            greet((tm + 2 * d, sp))

    for d in XS:
        greet(to_x[d])
    greet(other_core)
    for n in range(2, 5):
        loads[n].start()

    def column(h):
        return pl.ds(pl.multiple_of(h * hd, hd), hd)

    def span(g):
        first, count = GROUPS[g]
        return pl.ds(first, count)

    def send_x(g, d):
        return remote(part.at[d - 1, span(g)], from_x.at[d - 1, span(g)], x_send.at[g], x_recv.at[g], to_x[d])

    def all_x(g, send, recv):
        return remote(from_x.at[:, span(g)], from_x.at[:, span(g)], send.at[g], recv.at[g], to_x[1])

    def send_y(g, d):
        return remote(summed.at[span(g), rows_of[d]], from_y.at[d - 1, span(g)], y_send.at[g], y_recv.at[g], to_y[d])

    def all_y(g, send, recv):
        return remote(from_y.at[:, span(g)], from_y.at[:, span(g)], send.at[g], recv.at[g], to_y[1])

    def all_gx(g):
        piece = from_y.at[pl.ds(0, NX - 1), span(g)] if g in X_FIRST else from_x.at[:, span(g)]
        return remote(piece, piece, gx_send.at[g], gx_recv.at[g], to_x[1])

    def all_gy(g):
        piece = from_y.at[:, span(g)]
        if g in X_FIRST:
            piece = saved.at[pl.ds(0, NY - 1), :, pl.ds(0, GROUPS[g][1] * ROWS)]
        return remote(piece, piece, gy_send.at[g], gy_recv.at[g], to_y[1])

    def send_core(g):
        return remote(share.at[span(g)], from_core.at[span(g)], c_send.at[g], c_recv.at[g], other_core)

    def send_z(g, d):
        return remote(
            pair.at[span(g)], from_z.at[d - 1, span(g)], z_send.at[g, d - 1], z_recv.at[g, d - 1], (tm - 2 * d, sp)
        )

    def send_gy(g, d):
        piece = state.at[:, span(g), mine] if g in X_FIRST else state.at[x, span(g), mine]
        return remote(piece, piece, gy_send.at[g], gy_recv.at[g], to_y[d])

    def send_gx(g, d):
        piece = state.at[x, span(g), mine] if g in X_FIRST else state.at[x, span(g)]
        return remote(piece, piece, gx_send.at[g], gx_recv.at[g], to_x[d])

    def send_sy(d):
        piece = saved.at[y, x]
        return remote(piece, piece, s_send.at[0], s_recv.at[0], to_y[d])

    def send_sx(d):
        piece = saved.at[:, x]
        return remote(piece, piece, s_send.at[1], s_recv.at[1], to_x[d])

    def all_sy():
        piece = saved.at[pl.ds(0, NY - 1), 0]
        return remote(piece, piece, s_send.at[0], s_recv.at[0], to_y[1])

    def all_sx():
        piece = saved.at[:, pl.ds(0, NX - 1)]
        return remote(piece, piece, s_send.at[1], s_recv.at[1], to_x[1])

    def partial_states(g):
        first, count = GROUPS[g]
        for d in XS + (0,):
            for n in range(first, first + count):
                cols = column(x_at[d] * steps + n)
                product = tn(jnp.maximum(q[:, cols], 0), o[:, cols])
                if d:
                    part[d - 1, n] = product.astype(BF16)
                else:
                    own[n] = product

    loads[0].wait()
    loads[1].wait()
    for g in range(2):
        partial_states(g)
    pl.semaphore_wait(barrier, NX - 1 + 2 + 1 + z)

    for d in (1, 7):
        pl.semaphore_signal(ready.at[0], inc=1, device_id=to_y[d], device_id_type=MESH)
    for g in range(len(GROUPS)):
        if g >= 2:
            partial_states(g)
        for d in XS:
            send_x(g, d).start()
    loads[2].wait()
    for j in range(heads // 4):
        saved_rows = jnp.concatenate([s_rows[0, 4 * j + i].astype(F32) for i in range(4)], axis=0)
        saved[y, x, pl.ds(j * 16, 16), :] = saved_rows.astype(BF16)
    pl.semaphore_wait(ready.at[0], 2)
    for d in (2, 6):
        pl.semaphore_signal(ready.at[1], inc=1, device_id=to_y[d], device_id_type=MESH)

    row = lax.broadcasted_iota(jnp.int32, (hd, 4 * hd), 0)
    col = lax.broadcasted_iota(jnp.int32, (hd, 4 * hd), 1)
    target = (col // 16) * 4 + col % 4
    for i in range(4):
        hit = (row == target) & ((col // 4) % 4 == i)
        select[i] = jnp.where(hit, 1.0, 0.0).astype(BF16)

    pl.semaphore_wait(ready.at[1], 2)
    for d in RING:
        send_sy(d).start()


    for g, (first, count) in enumerate(GROUPS):
        all_x(g, x_send, x_recv).wait_recv()
        for n in range(first, first + count):
            total = own[n] + from_x[0, n].astype(F32) + from_x[1, n].astype(F32) + from_x[2, n].astype(F32)
            own[n] = total
            summed[n] = total.astype(BF16)
        for d in RING:
            send_y(g, d).start()

    all_sy().wait_recv()
    for d in XS:
        send_sx(d).start()

    def pass_down(g):
        send_core(g).wait_recv()
        ours, theirs = share[span(g)], from_core[span(g)]
        pair[span(g)] = (ours + theirs).astype(BF16)
        for d in RING:

            @pl.when(d <= z)
            def _(d=d):
                send_z(g, d).start()

        share_sum[span(g)] = ours + jnp.where(c == 0, theirs, 0.0)

    for g, (first, count) in enumerate(GROUPS):
        all_y(g, y_send, y_recv).wait_recv()
        for n in range(first, first + count):
            total = own[n, mine, :]
            for d in range(1, NY):
                total = total + from_y[d - 1, n].astype(F32)
            share[n] = total
        send_core(g).start()
        if g:
            pass_down(g - 1)
    pass_down(len(GROUPS) - 1)

    def query_grads(j):
        rows = saved[:, :, pl.ds(j * 16, 16), :].reshape(4 * hd, hd)
        for i in range(4):
            h = 4 * j + i
            cols = slice(h * hd, (h + 1) * hd)
            matrix = nn(select[i], rows).astype(BF16)
            product = nt(o[:, cols], matrix)
            dq[:, cols] = jnp.where(q[:, cols].astype(F32) > 0, product, 0.0).astype(BF16)

    all_sx().wait_recv()
    for j in range(heads // 4):
        query_grads(j)

    for g, (first, count) in enumerate(GROUPS):
        for d in range(1, NZ):

            @pl.when(d < NZ - z)
            def _(d=d, g=g):
                send_z(g, d).wait_recv()

        for n in range(first, first + count):
            total = share_sum[n]
            for d in range(1, NZ):
                total = total + jnp.where(d < NZ - z, from_z[d - 1, n].astype(F32), 0.0)
            state[x, n, mine, :] = (scale * total).astype(BF16)
        if g in X_FIRST:
            for d in XS:
                send_gx(g, d).start()
        else:
            for d in RING:
                send_gy(g, d).start()

    for g in range(len(GROUPS)):
        if g in X_FIRST:
            all_gx(g).wait_recv()
            for d in RING:
                send_gy(g, d).start()
        else:
            all_gy(g).wait_recv()
            for d in XS:
                send_gx(g, d).start()

    loads[3].wait()
    loads[4].wait()
    for g, (first, count) in enumerate(GROUPS):
        (all_gy if g in X_FIRST else all_gx)(g).wait_recv()
        for n in range(first, first + count):
            for m in range(NX):
                h = m * steps + n
                cols = slice(h * hd, (h + 1) * hd)
                matrix = state[m, n]
                keys = k[:, cols]
                product = nt(v[:, cols], matrix)
                dk[:, cols] = jnp.where(keys.astype(F32) > 0, product, 0.0).astype(BF16)
                dv[:, cols] = nn(jnp.maximum(keys, 0), matrix).astype(BF16)

    for g in range(len(GROUPS)):
        all_x(g, x_send, x_recv).wait_send()
        all_y(g, y_send, y_recv).wait_send()
        send_core(g).wait_send()
        for d in RING:

            @pl.when(d <= z)
            def _(d=d, g=g):
                send_z(g, d).wait_send()

        all_gy(g).wait_send()
        all_gx(g).wait_send()
    all_sy().wait_send()
    all_sx().wait_send()


def store(a, b, c, a_hbm, b_hbm, c_hbm, sem):
    copies = [
        pltpu.make_async_copy(src, dst, sem.at[n]) for n, (src, dst) in enumerate(((a, a_hbm), (b, b_hbm), (c, c_hbm)))
    ]
    for copy in copies:
        copy.start()
    for copy in copies:
        copy.wait()


def per_device(queries, keys, values, grad_out, saved_state):
    tok, width = queries.shape
    heads, hd = saved_state.shape[1], saved_state.shape[3]
    steps = heads // NX
    total_tok = tok * lax.axis_size("tm") * lax.axis_size("space")
    scale = 1.0 / math.sqrt(total_tok * hd)
    dma = pltpu.SemaphoreType.DMA
    vmem = pltpu.VMEM
    anywhere = pl.BlockSpec(memory_space=pl.ANY)
    local = pl.BlockSpec(memory_space=vmem)
    out = jax.ShapeDtypeStruct((tok, width), BF16)
    groups = len(GROUPS)
    grads = pl.pallas_call(
        functools.partial(kernel, scale),
        out_shape=(out, out, out),
        in_specs=[anywhere] * 5,
        out_specs=(local, local, local),
        scratch_shapes=[vmem((tok, width), BF16)] * 4
        + [
            vmem(saved_state.shape, BF16),
            vmem((NX - 1, steps, hd, hd), BF16),
            vmem((steps, hd, hd), F32),
            vmem((NX - 1, steps, hd, hd), BF16),
            vmem((steps, hd, hd), BF16),
            vmem((NY - 1, steps, ROWS, hd), BF16),
            vmem((steps, ROWS, hd), F32),
            vmem((steps, ROWS, hd), F32),
            vmem((steps, ROWS, hd), F32),
            vmem((steps, ROWS, hd), BF16),
            vmem((NZ - 1, steps, ROWS, hd), BF16),
            vmem((NX, steps, hd, hd), BF16),
            vmem((NY, NX, heads * 4, hd), BF16),
            vmem((4, hd, 4 * hd), BF16),
            dma((5,)),
            dma((groups,)),
            dma((groups,)),
            dma((groups,)),
            dma((groups,)),
            dma((groups,)),
            dma((groups,)),
            dma((groups, NZ - 1)),
            dma((groups, NZ - 1)),
            dma((groups,)),
            dma((groups,)),
            dma((groups,)),
            dma((groups,)),
            dma((2,)),
            dma((2,)),
            pltpu.SemaphoreType.REGULAR((2,)),
        ],
        compiler_params=pltpu.CompilerParams(
            collective_id=0, has_side_effects=True, vmem_limit_bytes=28000 * 1024
        ),
        name="state_grads",
    )(*(pltpu.with_memory_space_constraint(a, pltpu.HBM) for a in (queries, keys, values, grad_out, saved_state)))
    return pl.pallas_call(
        store,
        out_shape=(out, out, out),
        in_specs=[anywhere] * 3,
        out_specs=(anywhere, anywhere, anywhere),
        scratch_shapes=[dma((3,))],
        compiler_params=pltpu.CompilerParams(vmem_limit_bytes=1024 * 1024),
        name="store_grads",
    )(*grads)


def solution(mesh):
    rows = P(("tm", "space"), None)
    return jax.shard_map(
        per_device,
        mesh=mesh,
        in_specs=(rows, rows, rows, rows, P("tm", None, "space", None)),
        out_specs=(rows, rows, rows),
        check_vma=False,
    )
```

```python
import functools
import math

import jax
import jax.numpy as jnp
from jax import lax
from jax.experimental import pallas as pl
from jax.experimental.pallas import tpu as pltpu
from jax.sharding import PartitionSpec as P

MESH = pl.DeviceIdType.MESH
F32 = jnp.float32
BF16 = jnp.bfloat16
NX, NY, NZ = 4, 8, 8
ROWS = 16
X_FIRST = (1,)
GROUPS = ((0, 1), (1, 1), (2, 1), (3, 1), (4, 1))
XS = (2, 1, 3)
RING = (4, 3, 5, 2, 6, 1, 7)


def nt(a, b):
    return lax.dot_general(a, b, (((1,), (1,)), ((), ())), preferred_element_type=F32)


def tn(a, b):
    return lax.dot_general(a, b, (((0,), (0,)), ((), ())), preferred_element_type=F32)


def nn(a, b):
    return lax.dot_general(a, b, (((1,), (0,)), ((), ())), preferred_element_type=F32)


def kernel(
    scale,
    q_hbm,
    k_hbm,
    v_hbm,
    o_hbm,
    s_hbm,
    dq,
    dk,
    dv,
    q,
    k,
    v,
    o,
    s_rows,
    part,
    own,
    from_x,
    summed,
    from_y,
    share,
    share_sum,
    from_core,
    pair,
    from_z,
    state,
    saved,
    select,
    load_sem,
    x_send,
    x_recv,
    y_send,
    y_recv,
    c_send,
    c_recv,
    z_send,
    z_recv,
    gy_send,
    gy_recv,
    gx_send,
    gx_recv,
    s_send,
    s_recv,
):
    steps, hd = state.shape[1], state.shape[3]
    heads = NX * steps
    tm, sp = lax.axis_index("tm"), lax.axis_index("space")
    z, c = lax.div(tm, 2), lax.rem(tm, 2)
    y, x = lax.div(sp, NX), lax.rem(sp, NX)

    x_at = {d: lax.rem(x + d, NX) for d in range(NX)}
    y_at = {d: lax.rem(y + d, NY) for d in range(1, NY)}
    to_x = {d: (tm, y * NX + x_at[d]) for d in XS}
    to_y = {d: (tm, y_at[d] * NX + x) for d in RING}
    rows_of = {d: pl.ds(pl.multiple_of(y_at[d] * ROWS, ROWS), ROWS) for d in RING}
    mine = pl.ds(pl.multiple_of(y * ROWS, ROWS), ROWS)
    other_core = (tm + 1 - 2 * c, sp)

    def remote(src, dst, send, recv, device):
        return pltpu.make_async_remote_copy(
            src_ref=src, dst_ref=dst, send_sem=send, recv_sem=recv, device_id=device, device_id_type=MESH
        )

    barrier = pltpu.get_barrier_semaphore()

    def greet(device):
        pl.semaphore_signal(barrier, inc=1, device_id=device, device_id_type=MESH)

    loads = [
        pltpu.make_async_copy(src, dst, load_sem.at[n])
        for n, (src, dst) in enumerate(((q_hbm, q), (o_hbm, o), (s_hbm, s_rows), (k_hbm, k), (v_hbm, v)))
    ]
    loads[0].start()
    loads[1].start()
    for d in RING:
        greet(to_y[d])

        @pl.when(d < NZ - z)
        def _(d=d):
            greet((tm + 2 * d, sp))

    for d in XS:
        greet(to_x[d])
    greet(other_core)
    for n in range(2, 5):
        loads[n].start()

    def column(h):
        return pl.ds(pl.multiple_of(h * hd, hd), hd)

    def span(g):
        first, count = GROUPS[g]
        return pl.ds(first, count)

    def send_x(g, d):
        return remote(part.at[d - 1, span(g)], from_x.at[d - 1, span(g)], x_send.at[g], x_recv.at[g], to_x[d])

    def all_x(g, send, recv):
        return remote(from_x.at[:, span(g)], from_x.at[:, span(g)], send.at[g], recv.at[g], to_x[1])

    def send_y(g, d):
        return remote(summed.at[span(g), rows_of[d]], from_y.at[d - 1, span(g)], y_send.at[g], y_recv.at[g], to_y[d])

    def all_y(g, send, recv):
        return remote(from_y.at[:, span(g)], from_y.at[:, span(g)], send.at[g], recv.at[g], to_y[1])

    def all_gx(g):
        piece = from_y.at[pl.ds(0, NX - 1), span(g)] if g in X_FIRST else from_x.at[:, span(g)]
        return remote(piece, piece, gx_send.at[g], gx_recv.at[g], to_x[1])

    def all_gy(g):
        piece = from_y.at[:, span(g)]
        if g in X_FIRST:
            piece = saved.at[pl.ds(0, NY - 1), :, pl.ds(0, GROUPS[g][1] * ROWS)]
        return remote(piece, piece, gy_send.at[g], gy_recv.at[g], to_y[1])

    def send_core(g):
        return remote(share.at[span(g)], from_core.at[span(g)], c_send.at[g], c_recv.at[g], other_core)

    def send_z(g, d):
        return remote(
            pair.at[span(g)], from_z.at[d - 1, span(g)], z_send.at[g, d - 1], z_recv.at[g, d - 1], (tm - 2 * d, sp)
        )

    def send_gy(g, d):
        piece = state.at[:, span(g), mine] if g in X_FIRST else state.at[x, span(g), mine]
        return remote(piece, piece, gy_send.at[g], gy_recv.at[g], to_y[d])

    def send_gx(g, d):
        piece = state.at[x, span(g), mine] if g in X_FIRST else state.at[x, span(g)]
        return remote(piece, piece, gx_send.at[g], gx_recv.at[g], to_x[d])

    def send_sy(d):
        piece = saved.at[y, x]
        return remote(piece, piece, s_send.at[0], s_recv.at[0], to_y[d])

    def send_sx(d):
        piece = saved.at[:, x]
        return remote(piece, piece, s_send.at[1], s_recv.at[1], to_x[d])

    def all_sy():
        piece = saved.at[pl.ds(0, NY - 1), 0]
        return remote(piece, piece, s_send.at[0], s_recv.at[0], to_y[1])

    def all_sx():
        piece = saved.at[:, pl.ds(0, NX - 1)]
        return remote(piece, piece, s_send.at[1], s_recv.at[1], to_x[1])

    def partial_states(g):
        first, count = GROUPS[g]
        for d in XS + (0,):
            for n in range(first, first + count):
                cols = column(x_at[d] * steps + n)
                product = tn(jnp.maximum(q[:, cols], 0), o[:, cols])
                if d:
                    part[d - 1, n] = product.astype(BF16)
                else:
                    own[n] = product

    loads[0].wait()
    loads[1].wait()
    for g in range(len(GROUPS)):
        partial_states(g)
    loads[2].wait()
    for j in range(heads // 4):
        saved_rows = jnp.concatenate([s_rows[0, 4 * j + i].astype(F32) for i in range(4)], axis=0)
        saved[y, x, pl.ds(j * 16, 16), :] = saved_rows.astype(BF16)
    pl.semaphore_wait(barrier, NX - 1 + NY - 1 + 1 + z)
    for d in RING:
        send_sy(d).start()
    for g in range(len(GROUPS)):
        for d in XS:
            send_x(g, d).start()

    row = lax.broadcasted_iota(jnp.int32, (hd, 4 * hd), 0)
    col = lax.broadcasted_iota(jnp.int32, (hd, 4 * hd), 1)
    target = (col // 16) * 4 + col % 4
    for i in range(4):
        hit = (row == target) & ((col // 4) % 4 == i)
        select[i] = jnp.where(hit, 1.0, 0.0).astype(BF16)

    for g, (first, count) in enumerate(GROUPS):
        all_x(g, x_send, x_recv).wait_recv()
        for n in range(first, first + count):
            total = own[n] + from_x[0, n].astype(F32) + from_x[1, n].astype(F32) + from_x[2, n].astype(F32)
            own[n] = total
            summed[n] = total.astype(BF16)
        for d in RING:
            send_y(g, d).start()

    all_sy().wait_recv()
    for d in XS:
        send_sx(d).start()

    def pass_down(g):
        send_core(g).wait_recv()
        ours, theirs = share[span(g)], from_core[span(g)]
        pair[span(g)] = (ours + theirs).astype(BF16)
        for d in RING:

            @pl.when(d <= z)
            def _(d=d):
                send_z(g, d).start()

        share_sum[span(g)] = ours + jnp.where(c == 0, theirs, 0.0)

    for g, (first, count) in enumerate(GROUPS):
        all_y(g, y_send, y_recv).wait_recv()
        for n in range(first, first + count):
            total = own[n, mine, :]
            for d in range(1, NY):
                total = total + from_y[d - 1, n].astype(F32)
            share[n] = total
        send_core(g).start()
        if g:
            pass_down(g - 1)
    pass_down(len(GROUPS) - 1)

    def query_grads(j):
        rows = saved[:, :, pl.ds(j * 16, 16), :].reshape(4 * hd, hd)
        for i in range(4):
            h = 4 * j + i
            cols = slice(h * hd, (h + 1) * hd)
            matrix = nn(select[i], rows).astype(BF16)
            product = nt(o[:, cols], matrix)
            dq[:, cols] = jnp.where(q[:, cols].astype(F32) > 0, product, 0.0).astype(BF16)

    all_sx().wait_recv()
    for j in range(heads // 4):
        query_grads(j)

    for g, (first, count) in enumerate(GROUPS):
        for d in range(1, NZ):

            @pl.when(d < NZ - z)
            def _(d=d, g=g):
                send_z(g, d).wait_recv()

        for n in range(first, first + count):
            total = share_sum[n]
            for d in range(1, NZ):
                total = total + jnp.where(d < NZ - z, from_z[d - 1, n].astype(F32), 0.0)
            state[x, n, mine, :] = (scale * total).astype(BF16)
        if g in X_FIRST:
            for d in XS:
                send_gx(g, d).start()
        else:
            for d in RING:
                send_gy(g, d).start()

    for g in range(len(GROUPS)):
        if g in X_FIRST:
            all_gx(g).wait_recv()
            for d in RING:
                send_gy(g, d).start()
        else:
            all_gy(g).wait_recv()
            for d in XS:
                send_gx(g, d).start()

    loads[3].wait()
    loads[4].wait()
    for g, (first, count) in enumerate(GROUPS):
        (all_gy if g in X_FIRST else all_gx)(g).wait_recv()
        for n in range(first, first + count):
            for m in range(NX):
                h = m * steps + n
                cols = slice(h * hd, (h + 1) * hd)
                matrix = state[m, n]
                keys = k[:, cols]
                product = nt(v[:, cols], matrix)
                dk[:, cols] = jnp.where(keys.astype(F32) > 0, product, 0.0).astype(BF16)
                dv[:, cols] = nn(jnp.maximum(keys, 0), matrix).astype(BF16)

    for g in range(len(GROUPS)):
        all_x(g, x_send, x_recv).wait_send()
        all_y(g, y_send, y_recv).wait_send()
        send_core(g).wait_send()
        for d in RING:

            @pl.when(d <= z)
            def _(d=d, g=g):
                send_z(g, d).wait_send()

        all_gy(g).wait_send()
        all_gx(g).wait_send()
    all_sy().wait_send()
    all_sx().wait_send()


def store(a, b, c, a_hbm, b_hbm, c_hbm, sem):
    copies = [
        pltpu.make_async_copy(src, dst, sem.at[n]) for n, (src, dst) in enumerate(((a, a_hbm), (b, b_hbm), (c, c_hbm)))
    ]
    for copy in copies:
        copy.start()
    for copy in copies:
        copy.wait()


def per_device(queries, keys, values, grad_out, saved_state):
    tok, width = queries.shape
    heads, hd = saved_state.shape[1], saved_state.shape[3]
    steps = heads // NX
    total_tok = tok * lax.axis_size("tm") * lax.axis_size("space")
    scale = 1.0 / math.sqrt(total_tok * hd)
    dma = pltpu.SemaphoreType.DMA
    vmem = pltpu.VMEM
    anywhere = pl.BlockSpec(memory_space=pl.ANY)
    local = pl.BlockSpec(memory_space=vmem)
    out = jax.ShapeDtypeStruct((tok, width), BF16)
    groups = len(GROUPS)
    grads = pl.pallas_call(
        functools.partial(kernel, scale),
        out_shape=(out, out, out),
        in_specs=[anywhere] * 5,
        out_specs=(local, local, local),
        scratch_shapes=[vmem((tok, width), BF16)] * 4
        + [
            vmem(saved_state.shape, BF16),
            vmem((NX - 1, steps, hd, hd), BF16),
            vmem((steps, hd, hd), F32),
            vmem((NX - 1, steps, hd, hd), BF16),
            vmem((steps, hd, hd), BF16),
            vmem((NY - 1, steps, ROWS, hd), BF16),
            vmem((steps, ROWS, hd), F32),
            vmem((steps, ROWS, hd), F32),
            vmem((steps, ROWS, hd), F32),
            vmem((steps, ROWS, hd), BF16),
            vmem((NZ - 1, steps, ROWS, hd), BF16),
            vmem((NX, steps, hd, hd), BF16),
            vmem((NY, NX, heads * 4, hd), BF16),
            vmem((4, hd, 4 * hd), BF16),
            dma((5,)),
            dma((groups,)),
            dma((groups,)),
            dma((groups,)),
            dma((groups,)),
            dma((groups,)),
            dma((groups,)),
            dma((groups, NZ - 1)),
            dma((groups, NZ - 1)),
            dma((groups,)),
            dma((groups,)),
            dma((groups,)),
            dma((groups,)),
            dma((2,)),
            dma((2,)),
        ],
        compiler_params=pltpu.CompilerParams(
            collective_id=0, has_side_effects=True, vmem_limit_bytes=28000 * 1024
        ),
        name="state_grads",
    )(*(pltpu.with_memory_space_constraint(a, pltpu.HBM) for a in (queries, keys, values, grad_out, saved_state)))
    return pl.pallas_call(
        store,
        out_shape=(out, out, out),
        in_specs=[anywhere] * 3,
        out_specs=(anywhere, anywhere, anywhere),
        scratch_shapes=[dma((3,))],
        compiler_params=pltpu.CompilerParams(vmem_limit_bytes=1024 * 1024),
        name="store_grads",
    )(*grads)


def solution(mesh):
    rows = P(("tm", "space"), None)
    return jax.shard_map(
        per_device,
        mesh=mesh,
        in_specs=(rows, rows, rows, rows, P("tm", None, "space", None)),
        out_specs=(rows, rows, rows),
        check_vma=False,
    )
```

```python
import functools
import math

import jax
import jax.numpy as jnp
from jax import lax
from jax.experimental import pallas as pl
from jax.experimental.pallas import tpu as pltpu
from jax.sharding import PartitionSpec as P

MESH = pl.DeviceIdType.MESH
F32 = jnp.float32
BF16 = jnp.bfloat16
NX, NY, NZ = 4, 8, 8
ROWS = 16
X_FIRST = (3,)
GROUPS = ((0, 1), (1, 1), (2, 1), (3, 1), (4, 1))
XS = (2, 1, 3)
RING = (4, 3, 5, 2, 6, 1, 7)


def nt(a, b):
    return lax.dot_general(a, b, (((1,), (1,)), ((), ())), preferred_element_type=F32)


def tn(a, b):
    return lax.dot_general(a, b, (((0,), (0,)), ((), ())), preferred_element_type=F32)


def nn(a, b):
    return lax.dot_general(a, b, (((1,), (0,)), ((), ())), preferred_element_type=F32)


def kernel(
    scale,
    q_hbm,
    k_hbm,
    v_hbm,
    o_hbm,
    s_hbm,
    dq,
    dk,
    dv,
    q,
    k,
    v,
    o,
    s_rows,
    part,
    own,
    from_x,
    summed,
    from_y,
    share,
    share_sum,
    from_core,
    pair,
    from_z,
    state,
    saved,
    select,
    load_sem,
    x_send,
    x_recv,
    y_send,
    y_recv,
    c_send,
    c_recv,
    z_send,
    z_recv,
    gy_send,
    gy_recv,
    gx_send,
    gx_recv,
    s_send,
    s_recv,
):
    steps, hd = state.shape[1], state.shape[3]
    heads = NX * steps
    tm, sp = lax.axis_index("tm"), lax.axis_index("space")
    z, c = lax.div(tm, 2), lax.rem(tm, 2)
    y, x = lax.div(sp, NX), lax.rem(sp, NX)

    x_at = {d: lax.rem(x + d, NX) for d in range(NX)}
    y_at = {d: lax.rem(y + d, NY) for d in range(1, NY)}
    to_x = {d: (tm, y * NX + x_at[d]) for d in XS}
    to_y = {d: (tm, y_at[d] * NX + x) for d in RING}
    rows_of = {d: pl.ds(pl.multiple_of(y_at[d] * ROWS, ROWS), ROWS) for d in RING}
    mine = pl.ds(pl.multiple_of(y * ROWS, ROWS), ROWS)
    other_core = (tm + 1 - 2 * c, sp)

    def remote(src, dst, send, recv, device):
        return pltpu.make_async_remote_copy(
            src_ref=src, dst_ref=dst, send_sem=send, recv_sem=recv, device_id=device, device_id_type=MESH
        )

    barrier = pltpu.get_barrier_semaphore()

    def greet(device):
        pl.semaphore_signal(barrier, inc=1, device_id=device, device_id_type=MESH)

    loads = [
        pltpu.make_async_copy(src, dst, load_sem.at[n])
        for n, (src, dst) in enumerate(((q_hbm, q), (o_hbm, o), (s_hbm, s_rows), (k_hbm, k), (v_hbm, v)))
    ]
    loads[0].start()
    loads[1].start()
    for d in RING:
        greet(to_y[d])

        @pl.when(d < NZ - z)
        def _(d=d):
            greet((tm + 2 * d, sp))

    for d in XS:
        greet(to_x[d])
    greet(other_core)
    for n in range(2, 5):
        loads[n].start()

    def column(h):
        return pl.ds(pl.multiple_of(h * hd, hd), hd)

    def span(g):
        first, count = GROUPS[g]
        return pl.ds(first, count)

    def send_x(g, d):
        return remote(part.at[d - 1, span(g)], from_x.at[d - 1, span(g)], x_send.at[g], x_recv.at[g], to_x[d])

    def all_x(g, send, recv):
        return remote(from_x.at[:, span(g)], from_x.at[:, span(g)], send.at[g], recv.at[g], to_x[1])

    def send_y(g, d):
        return remote(summed.at[span(g), rows_of[d]], from_y.at[d - 1, span(g)], y_send.at[g], y_recv.at[g], to_y[d])

    def all_y(g, send, recv):
        return remote(from_y.at[:, span(g)], from_y.at[:, span(g)], send.at[g], recv.at[g], to_y[1])

    def all_gx(g):
        piece = from_y.at[pl.ds(0, NX - 1), span(g)] if g in X_FIRST else from_x.at[:, span(g)]
        return remote(piece, piece, gx_send.at[g], gx_recv.at[g], to_x[1])

    def all_gy(g):
        piece = from_y.at[:, span(g)]
        if g in X_FIRST:
            piece = saved.at[pl.ds(0, NY - 1), :, pl.ds(0, GROUPS[g][1] * ROWS)]
        return remote(piece, piece, gy_send.at[g], gy_recv.at[g], to_y[1])

    def send_core(g):
        return remote(share.at[span(g)], from_core.at[span(g)], c_send.at[g], c_recv.at[g], other_core)

    def send_z(g, d):
        return remote(
            pair.at[span(g)], from_z.at[d - 1, span(g)], z_send.at[g, d - 1], z_recv.at[g, d - 1], (tm - 2 * d, sp)
        )

    def send_gy(g, d):
        piece = state.at[:, span(g), mine] if g in X_FIRST else state.at[x, span(g), mine]
        return remote(piece, piece, gy_send.at[g], gy_recv.at[g], to_y[d])

    def send_gx(g, d):
        piece = state.at[x, span(g), mine] if g in X_FIRST else state.at[x, span(g)]
        return remote(piece, piece, gx_send.at[g], gx_recv.at[g], to_x[d])

    def send_sy(d):
        piece = saved.at[y, x]
        return remote(piece, piece, s_send.at[0], s_recv.at[0], to_y[d])

    def send_sx(d):
        piece = saved.at[:, x]
        return remote(piece, piece, s_send.at[1], s_recv.at[1], to_x[d])

    def all_sy():
        piece = saved.at[pl.ds(0, NY - 1), 0]
        return remote(piece, piece, s_send.at[0], s_recv.at[0], to_y[1])

    def all_sx():
        piece = saved.at[:, pl.ds(0, NX - 1)]
        return remote(piece, piece, s_send.at[1], s_recv.at[1], to_x[1])

    def partial_states(g):
        first, count = GROUPS[g]
        for d in XS + (0,):
            for n in range(first, first + count):
                cols = column(x_at[d] * steps + n)
                product = tn(jnp.maximum(q[:, cols], 0), o[:, cols])
                if d:
                    part[d - 1, n] = product.astype(BF16)
                else:
                    own[n] = product

    loads[0].wait()
    loads[1].wait()
    for g in range(len(GROUPS)):
        partial_states(g)
    loads[2].wait()
    for j in range(heads // 4):
        saved_rows = jnp.concatenate([s_rows[0, 4 * j + i].astype(F32) for i in range(4)], axis=0)
        saved[y, x, pl.ds(j * 16, 16), :] = saved_rows.astype(BF16)
    pl.semaphore_wait(barrier, NX - 1 + NY - 1 + 1 + z)
    for d in RING:
        send_sy(d).start()
    for g in range(len(GROUPS)):
        for d in XS:
            send_x(g, d).start()

    row = lax.broadcasted_iota(jnp.int32, (hd, 4 * hd), 0)
    col = lax.broadcasted_iota(jnp.int32, (hd, 4 * hd), 1)
    target = (col // 16) * 4 + col % 4
    for i in range(4):
        hit = (row == target) & ((col // 4) % 4 == i)
        select[i] = jnp.where(hit, 1.0, 0.0).astype(BF16)

    for g, (first, count) in enumerate(GROUPS):
        all_x(g, x_send, x_recv).wait_recv()
        for n in range(first, first + count):
            total = own[n] + from_x[0, n].astype(F32) + from_x[1, n].astype(F32) + from_x[2, n].astype(F32)
            own[n] = total
            summed[n] = total.astype(BF16)
        for d in RING:
            send_y(g, d).start()

    all_sy().wait_recv()
    for d in XS:
        send_sx(d).start()

    def pass_down(g):
        send_core(g).wait_recv()
        ours, theirs = share[span(g)], from_core[span(g)]
        pair[span(g)] = (ours + theirs).astype(BF16)
        for d in RING:

            @pl.when(d <= z)
            def _(d=d):
                send_z(g, d).start()

        share_sum[span(g)] = ours + jnp.where(c == 0, theirs, 0.0)

    for g, (first, count) in enumerate(GROUPS):
        all_y(g, y_send, y_recv).wait_recv()
        for n in range(first, first + count):
            total = own[n, mine, :]
            for d in range(1, NY):
                total = total + from_y[d - 1, n].astype(F32)
            share[n] = total
        send_core(g).start()
        if g:
            pass_down(g - 1)
    pass_down(len(GROUPS) - 1)

    def query_grads(j):
        rows = saved[:, :, pl.ds(j * 16, 16), :].reshape(4 * hd, hd)
        for i in range(4):
            h = 4 * j + i
            cols = slice(h * hd, (h + 1) * hd)
            matrix = nn(select[i], rows).astype(BF16)
            product = nt(o[:, cols], matrix)
            dq[:, cols] = jnp.where(q[:, cols].astype(F32) > 0, product, 0.0).astype(BF16)

    all_sx().wait_recv()
    for j in range(heads // 4):
        query_grads(j)

    for g, (first, count) in enumerate(GROUPS):
        for d in range(1, NZ):

            @pl.when(d < NZ - z)
            def _(d=d, g=g):
                send_z(g, d).wait_recv()

        for n in range(first, first + count):
            total = share_sum[n]
            for d in range(1, NZ):
                total = total + jnp.where(d < NZ - z, from_z[d - 1, n].astype(F32), 0.0)
            state[x, n, mine, :] = (scale * total).astype(BF16)
        if g in X_FIRST:
            for d in XS:
                send_gx(g, d).start()
        else:
            for d in RING:
                send_gy(g, d).start()

    for g in range(len(GROUPS)):
        if g in X_FIRST:
            all_gx(g).wait_recv()
            for d in RING:
                send_gy(g, d).start()
        else:
            all_gy(g).wait_recv()
            for d in XS:
                send_gx(g, d).start()

    loads[3].wait()
    loads[4].wait()
    for g, (first, count) in enumerate(GROUPS):
        (all_gy if g in X_FIRST else all_gx)(g).wait_recv()
        for n in range(first, first + count):
            for m in range(NX):
                h = m * steps + n
                cols = slice(h * hd, (h + 1) * hd)
                matrix = state[m, n]
                keys = k[:, cols]
                product = nt(v[:, cols], matrix)
                dk[:, cols] = jnp.where(keys.astype(F32) > 0, product, 0.0).astype(BF16)
                dv[:, cols] = nn(jnp.maximum(keys, 0), matrix).astype(BF16)

    for g in range(len(GROUPS)):
        all_x(g, x_send, x_recv).wait_send()
        all_y(g, y_send, y_recv).wait_send()
        send_core(g).wait_send()
        for d in RING:

            @pl.when(d <= z)
            def _(d=d, g=g):
                send_z(g, d).wait_send()

        all_gy(g).wait_send()
        all_gx(g).wait_send()
    all_sy().wait_send()
    all_sx().wait_send()


def store(a, b, c, a_hbm, b_hbm, c_hbm, sem):
    copies = [
        pltpu.make_async_copy(src, dst, sem.at[n]) for n, (src, dst) in enumerate(((a, a_hbm), (b, b_hbm), (c, c_hbm)))
    ]
    for copy in copies:
        copy.start()
    for copy in copies:
        copy.wait()


def per_device(queries, keys, values, grad_out, saved_state):
    tok, width = queries.shape
    heads, hd = saved_state.shape[1], saved_state.shape[3]
    steps = heads // NX
    total_tok = tok * lax.axis_size("tm") * lax.axis_size("space")
    scale = 1.0 / math.sqrt(total_tok * hd)
    dma = pltpu.SemaphoreType.DMA
    vmem = pltpu.VMEM
    anywhere = pl.BlockSpec(memory_space=pl.ANY)
    local = pl.BlockSpec(memory_space=vmem)
    out = jax.ShapeDtypeStruct((tok, width), BF16)
    groups = len(GROUPS)
    grads = pl.pallas_call(
        functools.partial(kernel, scale),
        out_shape=(out, out, out),
        in_specs=[anywhere] * 5,
        out_specs=(local, local, local),
        scratch_shapes=[vmem((tok, width), BF16)] * 4
        + [
            vmem(saved_state.shape, BF16),
            vmem((NX - 1, steps, hd, hd), BF16),
            vmem((steps, hd, hd), F32),
            vmem((NX - 1, steps, hd, hd), BF16),
            vmem((steps, hd, hd), BF16),
            vmem((NY - 1, steps, ROWS, hd), BF16),
            vmem((steps, ROWS, hd), F32),
            vmem((steps, ROWS, hd), F32),
            vmem((steps, ROWS, hd), F32),
            vmem((steps, ROWS, hd), BF16),
            vmem((NZ - 1, steps, ROWS, hd), BF16),
            vmem((NX, steps, hd, hd), BF16),
            vmem((NY, NX, heads * 4, hd), BF16),
            vmem((4, hd, 4 * hd), BF16),
            dma((5,)),
            dma((groups,)),
            dma((groups,)),
            dma((groups,)),
            dma((groups,)),
            dma((groups,)),
            dma((groups,)),
            dma((groups, NZ - 1)),
            dma((groups, NZ - 1)),
            dma((groups,)),
            dma((groups,)),
            dma((groups,)),
            dma((groups,)),
            dma((2,)),
            dma((2,)),
        ],
        compiler_params=pltpu.CompilerParams(
            collective_id=0, has_side_effects=True, vmem_limit_bytes=28000 * 1024
        ),
        name="state_grads",
    )(*(pltpu.with_memory_space_constraint(a, pltpu.HBM) for a in (queries, keys, values, grad_out, saved_state)))
    return pl.pallas_call(
        store,
        out_shape=(out, out, out),
        in_specs=[anywhere] * 3,
        out_specs=(anywhere, anywhere, anywhere),
        scratch_shapes=[dma((3,))],
        compiler_params=pltpu.CompilerParams(vmem_limit_bytes=1024 * 1024),
        name="store_grads",
    )(*grads)


def solution(mesh):
    rows = P(("tm", "space"), None)
    return jax.shard_map(
        per_device,
        mesh=mesh,
        in_specs=(rows, rows, rows, rows, P("tm", None, "space", None)),
        out_specs=(rows, rows, rows),
        check_vma=False,
    )
```
